1024 devices in a mesh: dp: 8 (over x, core), proto: 128 (over y, z).
Axes of the slice: x: 4, y: 4, z: 32, core: 2. Of those that a mesh axis runs over, the one named last changes fastest.
Arguments:
- student_rows: bfloat16 [10240, 256], P('dp'), may hold values from -0.5 to 0.5
- teacher_rows: bfloat16 [2048, 256], P('dp'), may hold values from -0.5 to 0.5
- prototypes: bfloat16 [256, 65536], P(None, 'proto'), may hold values from -0.375 to 0.375
- crop_image: int32 [10240], P('dp'), may hold values from 0 to 1023, as said below
- crop_global: int32 [10240], P('dp'), may hold values from 0 to 2, as said below
Outputs:
- student_grad: float32 [10240, 256], P('dp')
- proto_grad: float32 [256, 65536], P(None, 'proto')
The draws below stay inside these ranges and needn't reach their ends.
Inputs may be any that keep to these rules, and one draw needn't show every extreme that they name: `crop_image`: each image has exactly 10 crops; image i's crops all lie in rows of the aligned block of 1280 rows numbered i // 128, the block of dp that also holds its teacher rows. `crop_global`: for each image exactly one crop has each value 0 to 1 and the others have 2.
All inputs are finite; a program needn't handle non-finite values.
Results may differ from the reference program's by a relative error of at most 0.00065.
The reference program's roundings to bfloat16 on the way count: a program that leaves them out, or rounds other values in their place, can miss the bound.
Values may be sent and summed in bfloat16 or wider, within the bound.
No kernel may reach another device: no remote copies, remote signals or barrier semaphores. Data moves between devices by JAX's collectives and lax.ppermute only.
A program may use at most 32 MiB of HBM per device.

```python
import jax
import jax.numpy as jnp
from jax import lax

BOT = 256
IMG_DEV = 128
VIEWS = 10
GLOBALS = 2
ITERS = 3
PROTOS = 65536
IMAGES = 1024
CROPS = 10240
TEACH = 2048


def crop_layout(key):
    blocks = IMAGES // IMG_DEV
    block_rows = VIEWS * IMG_DEV
    keys = jax.random.split(key, blocks)
    slots = jax.vmap(lambda k: jax.random.permutation(k, block_rows))(keys)
    offset = (jnp.arange(blocks, dtype=jnp.int32) * IMG_DEV)[:, None]
    image = (offset + slots // VIEWS).reshape(-1).astype(jnp.int32)
    glob = jnp.minimum(slots % VIEWS, GLOBALS).reshape(-1).astype(jnp.int32)
    return (image, glob)


def draw_crop_image(key, part):
    return crop_layout(jax.random.fold_in(key, 7))[0]


def draw_crop_global(key, part):
    return crop_layout(jax.random.fold_in(key, 7))[1]


def level_of(key, shape, cuts, smallest, top_value):
    loudness, own = 1.0, jax.random.fold_in(key, 6)
    for axis_at, blocks in cuts:
        draws = jnp.exp(jax.random.uniform(jax.random.fold_in(own, axis_at), (blocks,), jnp.float32, smallest / len(cuts), top_value / len(cuts)))
        loudness = loudness * jnp.repeat(draws, shape[axis_at] // blocks).reshape([-1 if axis == axis_at else 1 for axis in range(len(shape))])
    return loudness


def bell_draw(rng, extent, width, bound, cuts=(), kind=jnp.bfloat16):
    entries = width * jax.random.normal(rng, extent, jnp.float32)
    if cuts:
        entries = entries * level_of(rng, extent, cuts, -0.22, 0.18)
    return jnp.clip(entries, -bound, bound).astype(kind)


def setup_inputs(seed: int = 0) -> dict:
    seeds = jax.random.split(jax.random.key(seed), 6)
    student_rows = bell_draw(seeds[0], (CROPS, BOT), 0.0625, 0.5, ((0, 8),))
    teacher_rows = bell_draw(seeds[1], (TEACH, BOT), 0.0625, 0.5, ((0, 8),))
    prototypes = bell_draw(seeds[2], (BOT, PROTOS), BOT ** -0.5, 0.375, ((1, 128),))
    crop_image = draw_crop_image(jax.random.fold_in(seeds[5], 71), 0)
    crop_global = draw_crop_global(jax.random.fold_in(seeds[5], 71), 0)
    return {"student_rows": student_rows, "teacher_rows": teacher_rows, "prototypes": prototypes, "crop_image": crop_image, "crop_global": crop_global}


def unit_rows(rows):
    scale = lax.rsqrt(lax.optimization_barrier(jnp.sum(rows * rows, axis=1, keepdims=True)) + 1e-06)
    return (rows * scale, scale)

def reference(student_rows, teacher_rows, prototypes, crop_image, crop_global):
    weights = prototypes.astype(jnp.float32)
    col_scale = lax.rsqrt(lax.optimization_barrier(jnp.sum(weights * weights, axis=0, keepdims=True)) + 1e-06)
    w_norm = weights * col_scale
    w_bf = w_norm.astype(jnp.bfloat16)
    t_norm, t_scale = unit_rows(teacher_rows.astype(jnp.float32))
    t_bf = t_norm.astype(jnp.bfloat16)
    q_mat = jnp.exp(jnp.dot(t_bf, w_bf, preferred_element_type=jnp.float32) / 0.07)
    for step in range(ITERS):
        q_mat = q_mat / lax.optimization_barrier(jnp.sum(q_mat, axis=0, keepdims=True)) / PROTOS
        q_mat = q_mat / lax.optimization_barrier(jnp.sum(q_mat, axis=1, keepdims=True)) / TEACH
    targets = q_mat * TEACH
    x_norm, x_scale = unit_rows(student_rows.astype(jnp.float32))
    x_bf = x_norm.astype(jnp.bfloat16)
    block_rows = VIEWS * IMG_DEV
    blocks = CROPS // block_rows
    scale_out = PROTOS / 64.0

    def one_block(carry, index):
        start = (index * block_rows).astype(jnp.int32)
        xb_blk = lax.dynamic_slice_in_dim(x_bf, start, block_rows, 0)
        xn_blk = lax.dynamic_slice_in_dim(x_norm, start, block_rows, 0)
        xr_blk = lax.dynamic_slice_in_dim(x_scale, start, block_rows, 0)
        image_blk = lax.dynamic_slice_in_dim(crop_image, start, block_rows, 0)
        glob_blk = lax.dynamic_slice_in_dim(crop_global, start, block_rows, 0)
        logits = jnp.dot(xb_blk, w_bf, preferred_element_type=jnp.float32) / 0.1
        expo = jnp.exp(logits)
        total = lax.optimization_barrier(jnp.sum(expo, axis=1, keepdims=True))
        probs = expo / total
        first = jnp.take(targets, GLOBALS * image_blk, axis=0)
        second = jnp.take(targets, GLOBALS * image_blk + 1, axis=0)
        keep_first = (glob_blk != 0).astype(jnp.float32)[:, None]
        keep_second = (glob_blk != 1).astype(jnp.float32)[:, None]
        target_blk = first * keep_first + second * keep_second
        count = keep_first + keep_second
        grad_bf = (scale_out * (count * probs - target_blk) / 0.1).astype(jnp.bfloat16)
        dxn = lax.dot_general(grad_bf, w_bf, (((1,), (1,)), ((), ())), preferred_element_type=jnp.float32)
        dx_blk = xr_blk * (dxn - xn_blk * lax.optimization_barrier(jnp.sum(xn_blk * dxn, axis=1, keepdims=True)))
        dwn = lax.dot_general(xb_blk, grad_bf, (((0,), (0,)), ((), ())), preferred_element_type=jnp.float32)
        return (carry + dwn, dx_blk)
    dwn_total, dx_all = lax.scan(one_block, jnp.zeros((BOT, PROTOS), jnp.float32), jnp.arange(blocks, dtype=jnp.int32))
    student_grad = dx_all.reshape(CROPS, BOT)
    proto_grad = col_scale * (dwn_total - w_norm * lax.optimization_barrier(jnp.sum(w_norm * dwn_total, axis=0, keepdims=True)))
    return (student_grad, proto_grad)
```

```python
import jax
import jax.numpy as jnp
from jax import lax
from jax.sharding import Mesh, PartitionSpec as P

GLOBALS = 2
ITERS = 3
DP = ("x", "core")
PROTO = ("y", "z")


def unit_rows(rows):
    scale = lax.rsqrt(jnp.sum(rows * rows, axis=1, keepdims=True) + 1e-06)
    return (rows * scale, scale)


def gather_sum(part, axes):
    return jnp.sum(lax.all_gather(part.reshape(-1, 128), axes, axis=0), axis=0).reshape(-1)


def hop_sum(part, axis, shifts):
    n = lax.axis_size(axis)
    got = [lax.ppermute(part, axis, [(i, (i + d) % n) for i in range(n)]) for d in shifts]
    for other in got:
        part = part + other
    return part


def on_device(student_rows, teacher_rows, prototypes, crop_image, crop_global):
    total_protos = lax.axis_size(PROTO) * prototypes.shape[1]
    img_local = teacher_rows.shape[0] // GLOBALS
    teach_total = lax.axis_size(DP) * teacher_rows.shape[0]
    weights = prototypes.astype(jnp.float32)
    col_scale = lax.rsqrt(jnp.sum(weights * weights, axis=0, keepdims=True) + 1e-06)
    w_norm = weights * col_scale
    w_bf = w_norm.astype(jnp.bfloat16)
    t_norm, t_scale = unit_rows(teacher_rows.astype(jnp.float32))
    t_bf = t_norm.astype(jnp.bfloat16)
    x_norm, x_scale = unit_rows(student_rows.astype(jnp.float32))
    x_bf = x_norm.astype(jnp.bfloat16)
    logits = jnp.dot(x_bf, w_bf, preferred_element_type=jnp.float32) / 0.1
    expo = jnp.exp(logits)
    part_total = jnp.sum(expo, axis=1)
    q_mat = jnp.exp(jnp.dot(t_bf, w_bf, preferred_element_type=jnp.float32) / 0.07)
    for step in range(ITERS):
        part_col = jnp.sum(q_mat, axis=0)
        if step == 0:
            col_tot = gather_sum(part_col, DP)
        elif step == 1:
            col_tot = gather_sum(gather_sum(part_col, ("core",)), ("x",))
        else:
            col_tot = hop_sum(hop_sum(part_col, "core", [1]), "x", [1, 2, 3])
        q_mat = q_mat / col_tot[None, :] / total_protos
        part_row = jnp.sum(q_mat, axis=1)
        if step == 0:
            both = gather_sum(jnp.concatenate([part_row, part_total]), PROTO)
            row_tot, total = both[: part_row.shape[0]], both[part_row.shape[0]:]
        elif step == 1:
            row_tot = gather_sum(gather_sum(part_row, ("y",)), ("z",))
        else:
            row_tot = hop_sum(part_row, "y", [1, 2, 3])
            row_tot = hop_sum(row_tot, "z", [1, 2, 3])
            row_tot = hop_sum(row_tot, "z", [4 * k for k in range(1, 8)])
        q_mat = q_mat / row_tot[:, None] / teach_total
    targets = q_mat * teach_total
    probs = expo / total[:, None]
    image_here = crop_image - lax.axis_index(DP) * img_local
    first = jnp.take(targets, GLOBALS * image_here, axis=0)
    second = jnp.take(targets, GLOBALS * image_here + 1, axis=0)
    keep_first = (crop_global != 0).astype(jnp.float32)[:, None]
    keep_second = (crop_global != 1).astype(jnp.float32)[:, None]
    target_rows = first * keep_first + second * keep_second
    count = keep_first + keep_second
    scale_out = total_protos / 64.0
    grad_bf = (scale_out * (count * probs - target_rows) / 0.1).astype(jnp.bfloat16)
    dxn_part = lax.dot_general(
        grad_bf, w_bf, (((1,), (1,)), ((), ())), preferred_element_type=jnp.float32
    )
    dwn_part = lax.dot_general(
        x_bf, grad_bf, (((0,), (0,)), ((), ())), preferred_element_type=jnp.float32
    )
    def reduce_all(part, axes):
        n = lax.axis_size(axes)
        pieces = part.reshape(n, part.shape[0] // n, part.shape[1])
        mine = jnp.sum(lax.all_to_all(pieces, axes, 0, 0), axis=0)
        return lax.all_gather(mine, axes, axis=0, tiled=True)

    dxn = reduce_all(dxn_part, PROTO)
    student_grad = x_scale * (dxn - x_norm * jnp.sum(x_norm * dxn, axis=1, keepdims=True))
    dwn_total = reduce_all(dwn_part, DP)
    proto_grad = col_scale * (
        dwn_total - w_norm * jnp.sum(w_norm * dwn_total, axis=0, keepdims=True)
    )
    return (student_grad, proto_grad)


def solution(mesh):
    nx, ny = 4, 4
    dp, proto = mesh.devices.shape
    fine = Mesh(mesh.devices.reshape(nx, dp // nx, ny, proto // ny), ("x", "core", "y", "z"))
    placed = (P(DP, None), P(DP, None), P(None, PROTO), P(DP), P(DP))
    return jax.shard_map(
        on_device,
        mesh=fine,
        in_specs=placed,
        out_specs=(P(DP, None), P(None, PROTO)),
        check_vma=False,
    )
```

```python
import jax
import jax.numpy as jnp
from jax import lax
from jax.sharding import Mesh, PartitionSpec as P

GLOBALS = 2
ITERS = 3
DP = ("x", "core")
PROTO = ("y", "zh", "zl")
ALONG = ("zh", "zl")


def unit_rows(rows):
    scale = lax.rsqrt(jnp.sum(rows * rows, axis=1, keepdims=True) + 1e-06)
    return (rows * scale, scale)


def spread(part, axes):
    n = lax.axis_size(axes)
    return lax.all_to_all(jnp.broadcast_to(part[None], (n,) + part.shape), axes, 0, 0)


def swap(part, axes):
    n = lax.axis_size(axes)
    pieces = part.reshape((n, part.shape[0] // n) + part.shape[1:])
    return lax.all_to_all(pieces, axes, 0, 0)


def spread_sum(part, *stages):
    rows = part.reshape(-1, 128)
    for axes in stages:
        rows = jnp.sum(spread(rows, axes), axis=0)
    return rows.reshape(-1)


def on_device(student_rows, teacher_rows, prototypes, crop_image, crop_global):
    total_protos = lax.axis_size(PROTO) * prototypes.shape[1]
    img_local = teacher_rows.shape[0] // GLOBALS
    teach_total = lax.axis_size(DP) * teacher_rows.shape[0]
    weights = prototypes.astype(jnp.float32)
    col_scale = lax.rsqrt(jnp.sum(weights * weights, axis=0, keepdims=True) + 1e-06)
    w_norm = weights * col_scale
    w_bf = w_norm.astype(jnp.bfloat16)
    t_norm, t_scale = unit_rows(teacher_rows.astype(jnp.float32))
    t_bf = t_norm.astype(jnp.bfloat16)
    x_norm, x_scale = unit_rows(student_rows.astype(jnp.float32))
    x_bf = x_norm.astype(jnp.bfloat16)
    logits = jnp.dot(x_bf, w_bf, preferred_element_type=jnp.float32) / 0.1
    expo = jnp.exp(logits)
    part_total = jnp.sum(expo, axis=1)
    q_mat = jnp.exp(jnp.dot(t_bf, w_bf, preferred_element_type=jnp.float32) / 0.07)
    n_teach, n_crop, ny = t_bf.shape[0], x_bf.shape[0], lax.axis_size("y")
    for step in range(ITERS):
        part_col = jnp.sum(q_mat, axis=0)
        if step == 1:
            col_tot = spread_sum(part_col, "core", "x")
        else:
            col_tot = spread_sum(part_col, DP)
        q_mat = q_mat / col_tot[None, :] / total_protos
        part_row = jnp.sum(q_mat, axis=1)
        if step == 0:
            own = jnp.pad(part_total.reshape(ny, -1), ((0, 0), (0, -(n_crop // ny) % 128)))
            row_ny = jnp.broadcast_to(part_row[None], (ny, n_teach))
            sent = jnp.concatenate([row_ny, own], axis=1).reshape(ny, -1, 128)
            both = spread_sum(jnp.sum(lax.all_to_all(sent, "y", 0, 0), axis=0), ALONG)
            row_tot, own_total = both[:n_teach], both[n_teach:]
        elif step == 1:
            both = spread(jnp.concatenate([part_row, own_total]).reshape(-1, 128), "y")
            both = both.reshape(ny, -1)
            total = both[:, n_teach : n_teach + n_crop // ny].reshape(-1)
            row_tot = spread_sum(jnp.sum(both[:, :n_teach], axis=0), "zl", "zh")
        else:
            row_tot = spread_sum(part_row, PROTO)
        q_mat = q_mat / row_tot[:, None] / teach_total
    targets = q_mat * teach_total
    probs = expo / total[:, None]
    image_here = crop_image - lax.axis_index(DP) * img_local
    first = jnp.take(targets, GLOBALS * image_here, axis=0)
    second = jnp.take(targets, GLOBALS * image_here + 1, axis=0)
    keep_first = (crop_global != 0).astype(jnp.float32)[:, None]
    keep_second = (crop_global != 1).astype(jnp.float32)[:, None]
    target_rows = first * keep_first + second * keep_second
    count = keep_first + keep_second
    scale_out = total_protos / 64.0
    grad_bf = (scale_out * (count * probs - target_rows) / 0.1).astype(jnp.bfloat16)
    dxn_part = lax.dot_general(
        grad_bf, w_bf, (((1,), (1,)), ((), ())), preferred_element_type=jnp.float32
    )
    dwn_part = lax.dot_general(
        x_bf, grad_bf, (((0,), (0,)), ((), ())), preferred_element_type=jnp.float32
    )
    dxn = dxn_part
    for axes in ("y", "zl", "zh"):
        dxn = jnp.sum(swap(dxn, axes), axis=0)
    for axes in ("zh", "zl", "y"):
        dxn = spread(dxn, axes).reshape(-1, dxn.shape[1])
    student_grad = x_scale * (dxn - x_norm * jnp.sum(x_norm * dxn, axis=1, keepdims=True))
    dwn_total = lax.all_gather(jnp.sum(swap(dwn_part, DP), axis=0), DP, axis=0, tiled=True)
    proto_grad = col_scale * (
        dwn_total - w_norm * jnp.sum(w_norm * dwn_total, axis=0, keepdims=True)
    )
    return (student_grad, proto_grad)


def solution(mesh):
    nx, ny, nzl = 4, 4, 4
    dp, proto = mesh.devices.shape
    split = (nx, dp // nx, ny, proto // ny // nzl, nzl)
    fine = Mesh(mesh.devices.reshape(split), ("x", "core", "y", "zh", "zl"))
    placed = (P(DP, None), P(DP, None), P(None, PROTO), P(DP), P(DP))
    return jax.shard_map(
        on_device,
        mesh=fine,
        in_specs=placed,
        out_specs=(P(DP, None), P(None, PROTO)),
        check_vma=False,
    )
```

```python
import jax
import jax.numpy as jnp
from jax import lax
from jax.sharding import Mesh, PartitionSpec as P

GLOBALS = 2
ITERS = 3
DP = ("x", "core")
PROTO = ("y", "zh", "zl")
NEAR = ("y", "zl")


def unit_rows(rows):
    scale = lax.rsqrt(jnp.sum(rows * rows, axis=1, keepdims=True) + 1e-06)
    return (rows * scale, scale)


def spread(part, axes):
    n = lax.axis_size(axes)
    return lax.all_to_all(jnp.broadcast_to(part[None], (n,) + part.shape), axes, 0, 0)


def swap(part, axes):
    n = lax.axis_size(axes)
    pieces = part.reshape((n, part.shape[0] // n) + part.shape[1:])
    return lax.all_to_all(pieces, axes, 0, 0)


def spread_sum(part, *stages):
    rows = part.reshape(-1, 128)
    for axes in stages:
        rows = jnp.sum(spread(rows, axes), axis=0)
    return rows.reshape(-1)


def on_device(student_rows, teacher_rows, prototypes, crop_image, crop_global):
    total_protos = lax.axis_size(PROTO) * prototypes.shape[1]
    img_local = teacher_rows.shape[0] // GLOBALS
    teach_total = lax.axis_size(DP) * teacher_rows.shape[0]
    weights = prototypes.astype(jnp.float32)
    col_scale = lax.rsqrt(jnp.sum(weights * weights, axis=0, keepdims=True) + 1e-06)
    w_norm = weights * col_scale
    w_bf = w_norm.astype(jnp.bfloat16)
    t_norm, t_scale = unit_rows(teacher_rows.astype(jnp.float32))
    t_bf = t_norm.astype(jnp.bfloat16)
    x_norm, x_scale = unit_rows(student_rows.astype(jnp.float32))
    x_bf = x_norm.astype(jnp.bfloat16)
    logits = jnp.dot(x_bf, w_bf, preferred_element_type=jnp.float32) / 0.1
    expo = jnp.exp(logits)
    part_total = jnp.sum(expo, axis=1)
    q_mat = jnp.exp(jnp.dot(t_bf, w_bf, preferred_element_type=jnp.float32) / 0.07)
    n_teach, n_crop, near = t_bf.shape[0], x_bf.shape[0], lax.axis_size(NEAR)
    own_crops = n_crop // near
    image_here = crop_image - lax.axis_index(DP) * img_local
    keep_first = (crop_global != 0).astype(jnp.float32)[:, None]
    keep_second = (crop_global != 1).astype(jnp.float32)[:, None]
    for step in range(ITERS):
        part_col = jnp.sum(q_mat, axis=0)
        q_mat = q_mat / spread_sum(part_col, DP)[None, :] / total_protos
        part_row = jnp.sum(q_mat, axis=1)
        if step == 0:
            own = jnp.pad(part_total.reshape(near, -1), ((0, 0), (0, -own_crops % 128)))
            rows = jnp.broadcast_to(part_row[None], (near, n_teach))
            sent = jnp.concatenate([rows, own], axis=1).reshape(near, -1, 128)
            both = spread_sum(jnp.sum(lax.all_to_all(sent, NEAR, 0, 0), axis=0), "zh")
            row_tot, own_total = both[:n_teach], both[n_teach:]
        elif step == 1:
            both = spread(jnp.concatenate([part_row, own_total]).reshape(-1, 128), NEAR)
            both = both.reshape(near, -1)
            total = both[:, n_teach : n_teach + own_crops].reshape(-1)
            row_tot = spread_sum(jnp.sum(both[:, :n_teach], axis=0), "zh")
        else:
            first = jnp.take(q_mat, GLOBALS * image_here, axis=0)
            second = jnp.take(q_mat, GLOBALS * image_here + 1, axis=0)
            row_tot = spread_sum(part_row, NEAR, "zh")
        if step + 1 < ITERS:
            q_mat = q_mat / row_tot[:, None] / teach_total
    teach_ids = lax.broadcasted_iota(jnp.int32, (1, n_teach), 1)

    def of_crop(index):
        return jnp.sum(jnp.where(index[:, None] == teach_ids, row_tot[None], 0.0), axis=1)

    first = first / of_crop(GLOBALS * image_here)[:, None] / teach_total * teach_total
    second = second / of_crop(GLOBALS * image_here + 1)[:, None] / teach_total * teach_total
    probs = expo / total[:, None]
    target_rows = first * keep_first + second * keep_second
    count = keep_first + keep_second
    scale_out = total_protos / 64.0
    grad_bf = (scale_out * (count * probs - target_rows) / 0.1).astype(jnp.bfloat16)
    dwn_part = lax.dot_general(
        x_bf, grad_bf, (((0,), (0,)), ((), ())), preferred_element_type=jnp.float32
    )
    dxn = lax.dot_general(
        grad_bf, w_bf, (((1,), (1,)), ((), ())), preferred_element_type=jnp.float32
    )
    dwn_total = spread(jnp.sum(swap(dwn_part, DP), axis=0), DP).reshape(dwn_part.shape)
    for axes in (NEAR, "zh"):
        dxn = jnp.sum(swap(dxn, axes), axis=0)
    for axes in ("zh", NEAR):
        dxn = spread(dxn, axes).reshape(-1, dxn.shape[1])
    student_grad = x_scale * (dxn - x_norm * jnp.sum(x_norm * dxn, axis=1, keepdims=True))
    proto_grad = col_scale * (
        dwn_total - w_norm * jnp.sum(w_norm * dwn_total, axis=0, keepdims=True)
    )
    return (student_grad, proto_grad)


def solution(mesh):
    nx, ny, nzl = 4, 4, 4
    dp, proto = mesh.devices.shape
    split = (nx, dp // nx, ny, proto // ny // nzl, nzl)
    fine = Mesh(mesh.devices.reshape(split), ("x", "core", "y", "zh", "zl"))
    placed = (P(DP, None), P(DP, None), P(None, PROTO), P(DP), P(DP))
    return jax.shard_map(
        on_device,
        mesh=fine,
        in_specs=placed,
        out_specs=(P(DP, None), P(None, PROTO)),
        check_vma=False,
    )
```

```python
import jax
import jax.numpy as jnp
from jax import lax
from jax.sharding import Mesh, PartitionSpec as P


GLOBALS = 2
ITERS = 3
DP = ("x", "core")
PROTO = ("y", "zh", "zl")
NEAR = ("y", "zl")


def unit_rows(rows):
    scale = lax.rsqrt(jnp.sum(rows * rows, axis=1, keepdims=True) + 1e-06)
    return (rows * scale, scale)


def spread(part, axes):
    n = lax.axis_size(axes)
    return lax.all_to_all(jnp.broadcast_to(part[None], (n,) + part.shape), axes, 0, 0)


def swap(part, axes):
    n = lax.axis_size(axes)
    pieces = part.reshape((n, part.shape[0] // n) + part.shape[1:])
    return lax.all_to_all(pieces, axes, 0, 0)


def spread_sum(part, *stages):
    rows = part.reshape(-1, 128)
    for axes in stages:
        rows = jnp.sum(spread(rows, axes), axis=0)
    return rows.reshape(-1)


def shifted(part, axis, step):
    n = lax.axis_size(axis)
    return lax.ppermute(part, axis, [(i, (i + step) % n) for i in range(n)])


def dwn_reduce(part):
    core, x, nx = lax.axis_index("core"), lax.axis_index("x"), lax.axis_size("x")
    half = part.shape[0] // 2
    piece = half // nx

    def rows(arr, start, size):
        return lax.dynamic_slice_in_dim(arr, start * size, size, 0)

    mine = rows(part, core, half) + shifted(rows(part, 1 - core, half), "core", 1)
    own = rows(mine, x, piece)
    for step in range(1, nx):
        own = own + shifted(rows(mine, (x + step) % nx, piece), "x", step)
    got = [own] + [shifted(own, "x", step) for step in range(1, nx)]
    back = got[:1] + got[:0:-1]
    start = (nx - x) % nx * piece
    mine = lax.dynamic_slice_in_dim(jnp.concatenate(back + back, axis=0), start, half, 0)
    other = shifted(mine, "core", 1)
    low, high = jnp.where(core == 0, mine, other), jnp.where(core == 0, other, mine)
    return jnp.concatenate([low, high], axis=0)


def on_device(student_rows, teacher_rows, prototypes, crop_image, crop_global):
    total_protos = lax.axis_size(PROTO) * prototypes.shape[1]
    img_local = teacher_rows.shape[0] // GLOBALS
    teach_total = lax.axis_size(DP) * teacher_rows.shape[0]
    weights = prototypes.astype(jnp.float32)
    col_scale = lax.rsqrt(jnp.sum(weights * weights, axis=0, keepdims=True) + 1e-06)
    w_norm = weights * col_scale
    w_bf = w_norm.astype(jnp.bfloat16)
    t_norm, _ = unit_rows(teacher_rows.astype(jnp.float32))
    t_bf = t_norm.astype(jnp.bfloat16)
    x_norm, x_scale = unit_rows(student_rows.astype(jnp.float32))
    x_bf = x_norm.astype(jnp.bfloat16)
    logits = jnp.dot(x_bf, w_bf, preferred_element_type=jnp.float32) / 0.1
    expo = jnp.exp(logits)
    part_total = jnp.sum(expo, axis=1)
    q_mat = jnp.exp(jnp.dot(t_bf, w_bf, preferred_element_type=jnp.float32) / 0.07)
    n_teach, n_crop, near = t_bf.shape[0], x_bf.shape[0], lax.axis_size(NEAR)
    own_crops = n_crop // near
    image_here = crop_image - lax.axis_index(DP) * img_local
    keep_first = (crop_global != 0).astype(jnp.float32)[:, None]
    keep_second = (crop_global != 1).astype(jnp.float32)[:, None]
    for step in range(ITERS):
        part_col = jnp.sum(q_mat, axis=0)
        q_mat = q_mat / spread_sum(part_col, DP)[None, :] / total_protos
        part_row = jnp.sum(q_mat, axis=1)
        if step == 0:
            own = jnp.pad(part_total.reshape(near, -1), ((0, 0), (0, -own_crops % 128)))
            rows = jnp.broadcast_to(part_row[None], (near, n_teach))
            sent = jnp.concatenate([rows, own], axis=1).reshape(near, -1, 128)
            both = spread_sum(jnp.sum(lax.all_to_all(sent, NEAR, 0, 0), axis=0), "zh")
            row_tot, own_total = both[:n_teach], both[n_teach:]
        elif step == 1:
            both = spread(jnp.concatenate([part_row, own_total]).reshape(-1, 128), NEAR)
            both = both.reshape(near, -1)
            total = both[:, n_teach : n_teach + own_crops].reshape(-1)
            row_tot = spread_sum(jnp.sum(both[:, :n_teach], axis=0), "zh")
        else:
            first = jnp.take(q_mat, GLOBALS * image_here, axis=0)
            second = jnp.take(q_mat, GLOBALS * image_here + 1, axis=0)
            row_tot = spread_sum(part_row, NEAR, "zh")
        if step + 1 < ITERS:
            q_mat = q_mat / row_tot[:, None] / teach_total
    teach_ids = lax.broadcasted_iota(jnp.int32, (1, n_teach), 1)

    def of_crop(index):
        return jnp.sum(jnp.where(index[:, None] == teach_ids, row_tot[None], 0.0), axis=1)

    first = first / of_crop(GLOBALS * image_here)[:, None] / teach_total * teach_total
    second = second / of_crop(GLOBALS * image_here + 1)[:, None] / teach_total * teach_total
    probs = expo / total[:, None]
    target_rows = first * keep_first + second * keep_second
    count = keep_first + keep_second
    scale_out = total_protos / 64.0
    grad_bf = (scale_out * (count * probs - target_rows) / 0.1).astype(jnp.bfloat16)
    dwn_part = lax.dot_general(
        x_bf, grad_bf, (((0,), (0,)), ((), ())), preferred_element_type=jnp.float32
    )
    dxn = lax.dot_general(
        grad_bf, w_bf, (((1,), (1,)), ((), ())), preferred_element_type=jnp.float32
    )
    dwn_total = dwn_reduce(dwn_part)
    for axes in ("y", "zl"):
        got = swap(dxn, axes)
        dxn = jnp.sum(got, axis=0)
    rows, lanes = dxn.shape[0], dxn.shape[1] // 2
    dxn = jnp.concatenate([dxn[:, :lanes], dxn[:, lanes:]], axis=0)
    got = swap(dxn, "zh")
    dxn = jnp.sum(got, axis=0)
    got = spread(dxn, "zh")
    dxn = got.reshape(-1, lanes)
    dxn = jnp.concatenate([dxn[:rows], dxn[rows:]], axis=1)
    for axes in ("zl", "y"):
        got = spread(dxn, axes)
        dxn = got.reshape(-1, dxn.shape[1])
    student_grad = x_scale * (dxn - x_norm * jnp.sum(x_norm * dxn, axis=1, keepdims=True))
    proto_grad = col_scale * (
        dwn_total - w_norm * jnp.sum(w_norm * dwn_total, axis=0, keepdims=True)
    )
    return (student_grad, proto_grad)


def solution(mesh):
    nx, ny, nzl = 4, 4, 4
    dp, proto = mesh.devices.shape
    split = (nx, dp // nx, ny, proto // ny // nzl, nzl)
    fine = Mesh(mesh.devices.reshape(split), ("x", "core", "y", "zh", "zl"))
    placed = (P(DP, None), P(DP, None), P(None, PROTO), P(DP), P(DP))

    return jax.shard_map(
        on_device,
        mesh=fine,
        in_specs=placed,
        out_specs=(P(DP, None), P(None, PROTO)),
        check_vma=False,
    )
```

```python
import jax
import jax.numpy as jnp
from jax import lax
from jax.sharding import Mesh, PartitionSpec as P


GLOBALS = 2
ITERS = 3
DP = ("x", "core")
PROTO = ("y", "zh", "zl")
NEAR = ("y", "zl")


def unit_rows(rows):
    scale = lax.rsqrt(jnp.sum(rows * rows, axis=1, keepdims=True) + 1e-06)
    return (rows * scale, scale)


def spread(part, axes):
    n = lax.axis_size(axes)
    return lax.all_to_all(jnp.broadcast_to(part[None], (n,) + part.shape), axes, 0, 0)


def swap(part, axes):
    n = lax.axis_size(axes)
    pieces = part.reshape((n, part.shape[0] // n) + part.shape[1:])
    return lax.all_to_all(pieces, axes, 0, 0)


def spread_sum(part, *stages):
    rows = part.reshape(-1, 128)
    for axes in stages:
        rows = jnp.sum(spread(rows, axes), axis=0)
    return rows.reshape(-1)


def shifted(part, axis, step):
    n = lax.axis_size(axis)
    return lax.ppermute(part, axis, [(i, (i + step) % n) for i in range(n)])


def dwn_reduce(part):
    core, x, nx = lax.axis_index("core"), lax.axis_index("x"), lax.axis_size("x")
    half = part.shape[0] // 2
    piece = half // nx

    def rows(arr, start, size):
        return lax.dynamic_slice_in_dim(arr, start * size, size, 0)

    mine = rows(part, core, half) + shifted(rows(part, 1 - core, half), "core", 1)
    sums = [rows(mine, x, piece)]
    for step in range(1, nx):
        sums.append(shifted(rows(mine, (x + step) % nx, piece), "x", step))
    own = lax.optimization_barrier(sum(sums[1:], sums[0]))
    got = [own] + [shifted(own, "x", step) for step in range(1, nx)]
    back = got[:1] + got[:0:-1]
    start = (nx - x) % nx * piece
    mine = lax.dynamic_slice_in_dim(jnp.concatenate(back + back, axis=0), start, half, 0)
    other = shifted(mine, "core", 1)
    low, high = jnp.where(core == 0, mine, other), jnp.where(core == 0, other, mine)
    return jnp.concatenate([low, high], axis=0)


def on_device(student_rows, teacher_rows, prototypes, crop_image, crop_global):
    total_protos = lax.axis_size(PROTO) * prototypes.shape[1]
    img_local = teacher_rows.shape[0] // GLOBALS
    teach_total = lax.axis_size(DP) * teacher_rows.shape[0]
    weights = prototypes.astype(jnp.float32)
    col_scale = lax.rsqrt(jnp.sum(weights * weights, axis=0, keepdims=True) + 1e-06)
    w_norm = weights * col_scale
    w_bf = w_norm.astype(jnp.bfloat16)
    t_norm, _ = unit_rows(teacher_rows.astype(jnp.float32))
    t_bf = t_norm.astype(jnp.bfloat16)
    x_norm, x_scale = unit_rows(student_rows.astype(jnp.float32))
    x_bf = x_norm.astype(jnp.bfloat16)
    logits = jnp.dot(x_bf, w_bf, preferred_element_type=jnp.float32) / 0.1
    expo = jnp.exp(logits)
    part_total = jnp.sum(expo, axis=1)
    q_mat = jnp.exp(jnp.dot(t_bf, w_bf, preferred_element_type=jnp.float32) / 0.07)
    n_teach, n_crop, near = t_bf.shape[0], x_bf.shape[0], lax.axis_size(NEAR)
    own_crops = n_crop // near
    image_here = crop_image - lax.axis_index(DP) * img_local
    keep_first = (crop_global != 0).astype(jnp.float32)[:, None]
    keep_second = (crop_global != 1).astype(jnp.float32)[:, None]
    for step in range(ITERS):
        part_col = jnp.sum(q_mat, axis=0)
        q_mat = q_mat / spread_sum(part_col, DP)[None, :] / total_protos
        part_row = jnp.sum(q_mat, axis=1)
        if step == 0:
            own = jnp.pad(part_total.reshape(near, -1), ((0, 0), (0, -own_crops % 128)))
            rows = jnp.broadcast_to(part_row[None], (near, n_teach))
            sent = jnp.concatenate([rows, own], axis=1).reshape(near, -1, 128)
            both = spread_sum(jnp.sum(lax.all_to_all(sent, NEAR, 0, 0), axis=0), "zh")
            row_tot, own_total = both[:n_teach], both[n_teach:]
        elif step == 1:
            both = spread(jnp.concatenate([part_row, own_total]).reshape(-1, 128), NEAR)
            both = both.reshape(near, -1)
            total = both[:, n_teach : n_teach + own_crops].reshape(-1)
            row_tot = spread_sum(jnp.sum(both[:, :n_teach], axis=0), "zh")
        else:
            first = jnp.take(q_mat, GLOBALS * image_here, axis=0)
            second = jnp.take(q_mat, GLOBALS * image_here + 1, axis=0)
            row_tot = spread_sum(part_row, NEAR, "zh")
        if step + 1 < ITERS:
            q_mat = q_mat / row_tot[:, None] / teach_total
    teach_ids = lax.broadcasted_iota(jnp.int32, (1, n_teach), 1)

    def of_crop(index):
        return jnp.sum(jnp.where(index[:, None] == teach_ids, row_tot[None], 0.0), axis=1)

    first = first / of_crop(GLOBALS * image_here)[:, None] / teach_total * teach_total
    second = second / of_crop(GLOBALS * image_here + 1)[:, None] / teach_total * teach_total
    probs = expo / total[:, None]
    target_rows = first * keep_first + second * keep_second
    count = keep_first + keep_second
    scale_out = total_protos / 64.0
    grad_bf = (scale_out * (count * probs - target_rows) / 0.1).astype(jnp.bfloat16)
    dwn_part = lax.dot_general(
        x_bf, grad_bf, (((0,), (0,)), ((), ())), preferred_element_type=jnp.float32
    )
    dxn = lax.dot_general(
        grad_bf, w_bf, (((1,), (1,)), ((), ())), preferred_element_type=jnp.float32
    )
    dwn_total = dwn_reduce(dwn_part)
    dxn = dxn - x_norm * jnp.sum(x_norm * dxn, axis=1, keepdims=True)
    got = swap(dxn.astype(jnp.float16), "y")
    dxn = jnp.sum(got.astype(jnp.float32), axis=0)
    got = swap(dxn, "zl")
    dxn = jnp.sum(got, axis=0)
    rows, lanes = dxn.shape[0], dxn.shape[1] // 2
    dxn = jnp.concatenate([dxn[:, :lanes], dxn[:, lanes:]], axis=0)
    got = swap(dxn, "zh")
    dxn = jnp.sum(got, axis=0).astype(jnp.float16)
    got = spread(dxn, "zh")
    dxn = got.reshape(-1, lanes)
    dxn = jnp.concatenate([dxn[:rows], dxn[rows:]], axis=1)
    for axes in ("zl", "y"):
        got = spread(dxn, axes)
        dxn = got.reshape(-1, dxn.shape[1])
    student_grad = x_scale * dxn.astype(jnp.float32)
    proto_grad = col_scale * (
        dwn_total - w_norm * jnp.sum(w_norm * dwn_total, axis=0, keepdims=True)
    )
    return (student_grad, proto_grad)


def solution(mesh):
    nx, ny, nzl = 4, 4, 4
    dp, proto = mesh.devices.shape
    split = (nx, dp // nx, ny, proto // ny // nzl, nzl)
    fine = Mesh(mesh.devices.reshape(split), ("x", "core", "y", "zh", "zl"))
    placed = (P(DP, None), P(DP, None), P(None, PROTO), P(DP), P(DP))

    return jax.shard_map(
        on_device,
        mesh=fine,
        in_specs=placed,
        out_specs=(P(DP, None), P(None, PROTO)),
        check_vma=False,
    )
```

```python
import jax
import jax.numpy as jnp
from jax import lax
from jax.sharding import Mesh, PartitionSpec as P


GLOBALS = 2
ITERS = 3
DP = ("x", "core")
PROTO = ("y", "zh", "zl")
NEAR = ("y", "zl")


def unit_rows(rows):
    scale = lax.rsqrt(jnp.sum(rows * rows, axis=1, keepdims=True) + 1e-06)
    return (rows * scale, scale)


def spread(part, axes):
    n = lax.axis_size(axes)
    return lax.all_to_all(jnp.broadcast_to(part[None], (n,) + part.shape), axes, 0, 0)


def swap(part, axes):
    n = lax.axis_size(axes)
    pieces = part.reshape((n, part.shape[0] // n) + part.shape[1:])
    return lax.all_to_all(pieces, axes, 0, 0)


def spread_sum(part, *stages):
    rows = part.reshape(-1, 128)
    for axes in stages:
        rows = jnp.sum(spread(rows, axes), axis=0)
    return rows.reshape(-1)


def shifted(part, axis, step):
    n = lax.axis_size(axis)
    return lax.ppermute(part, axis, [(i, (i + step) % n) for i in range(n)])


def dwn_reduce(part):
    core, x, nx = lax.axis_index("core"), lax.axis_index("x"), lax.axis_size("x")
    half = part.shape[0] // 2
    piece = half // nx

    def rows(arr, start, size):
        return lax.dynamic_slice_in_dim(arr, start * size, size, 0)

    mine = rows(part, core, half) + shifted(rows(part, 1 - core, half), "core", 1)
    sums = [rows(mine, x, piece)]
    for step in range(1, nx):
        sums.append(shifted(rows(mine, (x + step) % nx, piece), "x", step))
    own = lax.optimization_barrier(sum(sums[1:], sums[0]))
    got = [own] + [shifted(own, "x", step) for step in range(1, nx)]
    back = got[:1] + got[:0:-1]
    start = (nx - x) % nx * piece
    mine = lax.dynamic_slice_in_dim(jnp.concatenate(back + back, axis=0), start, half, 0)
    other = shifted(mine, "core", 1)
    low, high = jnp.where(core == 0, mine, other), jnp.where(core == 0, other, mine)
    return jnp.concatenate([low, high], axis=0)


def on_device(student_rows, teacher_rows, prototypes, crop_image, crop_global):
    total_protos = lax.axis_size(PROTO) * prototypes.shape[1]
    img_local = teacher_rows.shape[0] // GLOBALS
    teach_total = lax.axis_size(DP) * teacher_rows.shape[0]
    weights = prototypes.astype(jnp.float32)
    col_scale = lax.rsqrt(jnp.sum(weights * weights, axis=0, keepdims=True) + 1e-06)
    w_norm = weights * col_scale
    w_bf = w_norm.astype(jnp.bfloat16)
    t_norm, _ = unit_rows(teacher_rows.astype(jnp.float32))
    t_bf = t_norm.astype(jnp.bfloat16)
    x_norm, x_scale = unit_rows(student_rows.astype(jnp.float32))
    x_bf = x_norm.astype(jnp.bfloat16)
    logits = jnp.dot(x_bf, w_bf, preferred_element_type=jnp.float32) / 0.1
    expo = jnp.exp(logits)
    part_total = jnp.sum(expo, axis=1)
    q_mat = jnp.exp(jnp.dot(t_bf, w_bf, preferred_element_type=jnp.float32) / 0.07)
    n_teach, n_crop, near = t_bf.shape[0], x_bf.shape[0], lax.axis_size(NEAR)
    own_crops = n_crop // near
    image_here = crop_image - lax.axis_index(DP) * img_local
    keep_first = (crop_global != 0).astype(jnp.float32)[:, None]
    keep_second = (crop_global != 1).astype(jnp.float32)[:, None]
    for step in range(ITERS):
        part_col = jnp.sum(q_mat, axis=0)
        q_mat = q_mat / spread_sum(part_col, DP)[None, :] / total_protos
        part_row = jnp.sum(q_mat, axis=1)
        if step == 0:
            own = jnp.pad(part_total.reshape(near, -1), ((0, 0), (0, -own_crops % 128)))
            rows = jnp.broadcast_to(part_row[None], (near, n_teach))
            sent = jnp.concatenate([rows, own], axis=1).reshape(near, -1, 128)
            both = spread_sum(jnp.sum(lax.all_to_all(sent, NEAR, 0, 0), axis=0), "zh")
            row_tot, own_total = both[:n_teach], both[n_teach:]
        elif step == 1:
            both = spread(jnp.concatenate([part_row, own_total]).reshape(-1, 128), NEAR)
            both = both.reshape(near, -1)
            total = both[:, n_teach : n_teach + own_crops].reshape(-1)
            row_tot = spread_sum(jnp.sum(both[:, :n_teach], axis=0), "zh")
        else:
            first = jnp.take(q_mat, GLOBALS * image_here, axis=0)
            second = jnp.take(q_mat, GLOBALS * image_here + 1, axis=0)
            row_tot = spread_sum(part_row, NEAR, "zh")
        if step + 1 < ITERS:
            q_mat = q_mat / row_tot[:, None] / teach_total
    teach_ids = lax.broadcasted_iota(jnp.int32, (1, n_teach), 1)

    def of_crop(index):
        return jnp.sum(jnp.where(index[:, None] == teach_ids, row_tot[None], 0.0), axis=1)

    first = first / of_crop(GLOBALS * image_here)[:, None] / teach_total * teach_total
    second = second / of_crop(GLOBALS * image_here + 1)[:, None] / teach_total * teach_total
    probs = expo / total[:, None]
    target_rows = first * keep_first + second * keep_second
    count = keep_first + keep_second
    scale_out = total_protos / 64.0
    grad_bf = (scale_out * (count * probs - target_rows) / 0.1).astype(jnp.bfloat16)
    dwn_part = lax.dot_general(
        x_bf, grad_bf, (((0,), (0,)), ((), ())), preferred_element_type=jnp.float32
    )
    dxn = lax.dot_general(
        grad_bf, w_bf, (((1,), (1,)), ((), ())), preferred_element_type=jnp.float32
    )
    dwn_total = dwn_reduce(dwn_part)
    dxn = dxn - x_norm * jnp.sum(x_norm * dxn, axis=1, keepdims=True)
    got = swap(dxn.astype(jnp.float16), "y")
    dxn = jnp.sum(got.astype(jnp.float32), axis=0)
    got = swap(dxn.astype(jnp.float16), "zl")
    dxn = jnp.sum(got.astype(jnp.float32), axis=0)
    got = spread(dxn.astype(jnp.float16), "zh")
    dxn = jnp.sum(got.astype(jnp.float32), axis=0).astype(jnp.float16)
    for axes in ("zl", "y"):
        got = spread(dxn, axes)
        dxn = got.reshape(-1, dxn.shape[1])
    student_grad = x_scale * dxn.astype(jnp.float32)
    proto_grad = col_scale * (
        dwn_total - w_norm * jnp.sum(w_norm * dwn_total, axis=0, keepdims=True)
    )
    return (student_grad, proto_grad)


def solution(mesh):
    nx, ny, nzl = 4, 4, 4
    dp, proto = mesh.devices.shape
    split = (nx, dp // nx, ny, proto // ny // nzl, nzl)
    fine = Mesh(mesh.devices.reshape(split), ("x", "core", "y", "zh", "zl"))
    placed = (P(DP, None), P(DP, None), P(None, PROTO), P(DP), P(DP))

    return jax.shard_map(
        on_device,
        mesh=fine,
        in_specs=placed,
        out_specs=(P(DP, None), P(None, PROTO)),
        check_vma=False,
    )
```

```python
import jax
import jax.numpy as jnp
from jax import lax
from jax.sharding import Mesh, PartitionSpec as P


GLOBALS = 2
ITERS = 3
DP = ("x", "core")
PROTO = ("y", "zh", "zl")
NEAR = ("y", "zl")


def unit_rows(rows):
    scale = lax.rsqrt(jnp.sum(rows * rows, axis=1, keepdims=True) + 1e-06)
    return (rows * scale, scale)


def spread(part, axes):
    n = lax.axis_size(axes)
    return lax.all_to_all(jnp.broadcast_to(part[None], (n,) + part.shape), axes, 0, 0)


def swap(part, axes):
    n = lax.axis_size(axes)
    pieces = part.reshape((n, part.shape[0] // n) + part.shape[1:])
    return lax.all_to_all(pieces, axes, 0, 0)


def spread_sum(part, *stages):
    rows = part.reshape(-1, 128)
    for axes in stages:
        rows = jnp.sum(spread(rows, axes), axis=0)
    return rows.reshape(-1)


def shifted(part, axis, step):
    n = lax.axis_size(axis)
    return lax.ppermute(part, axis, [(i, (i + step) % n) for i in range(n)])


def dwn_reduce(part):
    core, x, nx = lax.axis_index("core"), lax.axis_index("x"), lax.axis_size("x")
    half = part.shape[0] // 2
    piece = half // nx

    def rows(arr, start, size):
        return lax.dynamic_slice_in_dim(arr, start * size, size, 0)

    mine = rows(part, core, half) + shifted(rows(part, 1 - core, half), "core", 1)
    sums = [rows(mine, x, piece)]
    for step in range(1, nx):
        sums.append(shifted(rows(mine, (x + step) % nx, piece), "x", step))
    own = lax.optimization_barrier(sum(sums[1:], sums[0]))
    got = [own] + [shifted(own, "x", step) for step in range(1, nx)]
    back = got[:1] + got[:0:-1]
    start = (nx - x) % nx * piece
    mine = lax.dynamic_slice_in_dim(jnp.concatenate(back + back, axis=0), start, half, 0)
    other = shifted(mine, "core", 1)
    low, high = jnp.where(core == 0, mine, other), jnp.where(core == 0, other, mine)
    return jnp.concatenate([low, high], axis=0)


def on_device(student_rows, teacher_rows, prototypes, crop_image, crop_global):
    total_protos = lax.axis_size(PROTO) * prototypes.shape[1]
    img_local = teacher_rows.shape[0] // GLOBALS
    teach_total = lax.axis_size(DP) * teacher_rows.shape[0]
    weights = prototypes.astype(jnp.float32)
    col_scale = lax.rsqrt(jnp.sum(weights * weights, axis=0, keepdims=True) + 1e-06)
    w_norm = weights * col_scale
    w_bf = w_norm.astype(jnp.bfloat16)
    t_norm, _ = unit_rows(teacher_rows.astype(jnp.float32))
    t_bf = t_norm.astype(jnp.bfloat16)
    x_norm, x_scale = unit_rows(student_rows.astype(jnp.float32))
    x_bf = x_norm.astype(jnp.bfloat16)
    logits = jnp.dot(x_bf, w_bf, preferred_element_type=jnp.float32) / 0.1
    expo = jnp.exp(logits)
    part_total = jnp.sum(expo, axis=1)
    q_mat = jnp.exp(jnp.dot(t_bf, w_bf, preferred_element_type=jnp.float32) / 0.07)
    n_teach, n_crop, near = t_bf.shape[0], x_bf.shape[0], lax.axis_size(NEAR)
    own_crops = n_crop // near
    image_here = crop_image - lax.axis_index(DP) * img_local
    first_at, second_at = GLOBALS * image_here, GLOBALS * image_here + 1
    keep_first = (crop_global != 0).astype(jnp.float32)
    keep_second = (crop_global != 1).astype(jnp.float32)
    prep = (first_at, second_at, keep_first, keep_second)
    first_at, second_at, keep_first, keep_second = lax.optimization_barrier(prep)
    keep_first, keep_second = keep_first[:, None], keep_second[:, None]
    for step in range(ITERS):
        part_col = jnp.sum(q_mat, axis=0)
        col_tot = spread_sum(part_col, DP)
        q_mat = q_mat / col_tot[None, :] / total_protos
        part_row = jnp.sum(q_mat, axis=1)
        if step == 0:
            own = jnp.pad(part_total.reshape(near, -1), ((0, 0), (0, -own_crops % 128)))
            rows = jnp.broadcast_to(part_row[None], (near, n_teach))
            sent = jnp.concatenate([rows, own], axis=1).reshape(near, -1, 128)
            both = spread_sum(jnp.sum(lax.all_to_all(sent, NEAR, 0, 0), axis=0), "zh")
            row_tot = both[:n_teach]
        elif step == 1:
            both, part_row = lax.optimization_barrier((both, part_row))
            sent = jnp.concatenate([part_row, both[n_teach:]])
            both = spread(sent.reshape(-1, 128), NEAR)
            near_row = jnp.sum(both.reshape(near, -1)[:, :n_teach], axis=0)
            row_tot = spread_sum(near_row, "zh")
        else:
            near_row = spread_sum(part_row, NEAR)
            late = (near_row, both, first_at, second_at)
            near_row, both, first_at, second_at = lax.optimization_barrier(late)
            total = both.reshape(near, -1)[:, n_teach : n_teach + own_crops].reshape(-1)
            first = q_mat.at[first_at].get(mode="promise_in_bounds")
            second = q_mat.at[second_at].get(mode="promise_in_bounds")
            row_tot = spread_sum(near_row, "zh")
        if step + 1 < ITERS:
            q_mat = q_mat / row_tot[:, None] / teach_total
    teach_ids = lax.broadcasted_iota(jnp.int32, (1, n_teach), 1)

    def of_crop(index):
        return jnp.sum(jnp.where(index[:, None] == teach_ids, row_tot[None], 0.0), axis=1)

    first = first / of_crop(first_at)[:, None] / teach_total * teach_total
    second = second / of_crop(second_at)[:, None] / teach_total * teach_total
    probs = expo / total[:, None]
    target_rows = first * keep_first + second * keep_second
    count = keep_first + keep_second
    scale_out = total_protos / 64.0
    grad_bf = (scale_out * (count * probs - target_rows) / 0.1).astype(jnp.bfloat16)
    dxn = lax.dot_general(
        grad_bf, w_bf, (((1,), (1,)), ((), ())), preferred_element_type=jnp.float32
    )
    dxn = dxn - x_norm * jnp.sum(x_norm * dxn, axis=1, keepdims=True)
    got = swap(dxn.astype(jnp.float16), "y")
    dxn = jnp.sum(got.astype(jnp.float32), axis=0)
    got = swap(dxn.astype(jnp.float16), "zl")
    dxn = jnp.sum(got.astype(jnp.float32), axis=0)
    dxn, grad_bf = lax.optimization_barrier((dxn, grad_bf))
    dwn_part = lax.dot_general(
        x_bf, grad_bf, (((0,), (0,)), ((), ())), preferred_element_type=jnp.float32
    )
    dwn_total = dwn_reduce(dwn_part)
    got = spread(dxn.astype(jnp.float16), "zh")
    dxn = jnp.sum(got.astype(jnp.float32), axis=0).astype(jnp.float16)
    for axes in ("zl", "y"):
        got = spread(dxn, axes)
        dxn = got.reshape(-1, dxn.shape[1])
    student_grad = x_scale * dxn.astype(jnp.float32)
    proto_grad = col_scale * (
        dwn_total - w_norm * jnp.sum(w_norm * dwn_total, axis=0, keepdims=True)
    )
    return (student_grad, proto_grad)


def solution(mesh):
    nx, ny, nzl = 4, 4, 4
    dp, proto = mesh.devices.shape
    split = (nx, dp // nx, ny, proto // ny // nzl, nzl)
    fine = Mesh(mesh.devices.reshape(split), ("x", "core", "y", "zh", "zl"))
    placed = (P(DP, None), P(DP, None), P(None, PROTO), P(DP), P(DP))

    return jax.shard_map(
        on_device,
        mesh=fine,
        in_specs=placed,
        out_specs=(P(DP, None), P(None, PROTO)),
        check_vma=False,
    )
```

```python
import jax
import jax.numpy as jnp
from jax import lax
from jax.sharding import Mesh, PartitionSpec as P


GLOBALS = 2
ITERS = 3
DP = ("x", "core")
PROTO = ("y", "zh", "zl")
NEAR = ("y", "zl")


def unit_rows(rows):
    scale = lax.rsqrt(jnp.sum(rows * rows, axis=1, keepdims=True) + 1e-06)
    return (rows * scale, scale)


def spread(part, axes):
    n = lax.axis_size(axes)
    return lax.all_to_all(jnp.broadcast_to(part[None], (n,) + part.shape), axes, 0, 0)


def swap(part, axes):
    n = lax.axis_size(axes)
    pieces = part.reshape((n, part.shape[0] // n) + part.shape[1:])
    return lax.all_to_all(pieces, axes, 0, 0)


def spread_sum(part, *stages):
    rows = part.reshape(-1, 128)
    for axes in stages:
        rows = jnp.sum(spread(rows, axes), axis=0)
    return rows.reshape(-1)


def shifted(part, axis, step):
    n = lax.axis_size(axis)
    return lax.ppermute(part, axis, [(i, (i + step) % n) for i in range(n)])


def dwn_reduce(part):
    core, x, nx = lax.axis_index("core"), lax.axis_index("x"), lax.axis_size("x")
    half = part.shape[0] // 2
    piece = half // nx

    def rows(arr, start, size):
        return lax.dynamic_slice_in_dim(arr, start * size, size, 0)

    mine = rows(part, core, half) + shifted(rows(part, 1 - core, half), "core", 1)
    sums = [rows(mine, x, piece)]
    for step in range(1, nx):
        sums.append(shifted(rows(mine, (x + step) % nx, piece), "x", step))
    own = lax.optimization_barrier(sum(sums[1:], sums[0]))
    got = [own] + [shifted(own, "x", step) for step in range(1, nx)]
    back = got[:1] + got[:0:-1]
    return jnp.concatenate(back + back, axis=0)


def dwn_join(ring):
    core, x, nx = lax.axis_index("core"), lax.axis_index("x"), lax.axis_size("x")
    half = ring.shape[0] // 2
    mine = lax.dynamic_slice_in_dim(ring, (nx - x) % nx * (half // nx), half, 0)
    other = shifted(mine, "core", 1)
    low, high = jnp.where(core == 0, mine, other), jnp.where(core == 0, other, mine)
    return jnp.concatenate([low, high], axis=0)


def on_device(student_rows, teacher_rows, prototypes, crop_image, crop_global):
    total_protos = lax.axis_size(PROTO) * prototypes.shape[1]
    img_local = teacher_rows.shape[0] // GLOBALS
    teach_total = lax.axis_size(DP) * teacher_rows.shape[0]
    weights = prototypes.astype(jnp.float32)
    col_scale = lax.rsqrt(jnp.sum(weights * weights, axis=0, keepdims=True) + 1e-06)
    w_norm = weights * col_scale
    w_bf = w_norm.astype(jnp.bfloat16)
    t_norm, _ = unit_rows(teacher_rows.astype(jnp.float32))
    t_bf = t_norm.astype(jnp.bfloat16)
    x_norm, x_scale = unit_rows(student_rows.astype(jnp.float32))
    x_bf = x_norm.astype(jnp.bfloat16)
    logits = jnp.dot(x_bf, w_bf, preferred_element_type=jnp.float32) / 0.1
    expo = jnp.exp(logits)
    part_total = jnp.sum(expo, axis=1)
    q_mat = jnp.exp(jnp.dot(t_bf, w_bf, preferred_element_type=jnp.float32) / 0.07)
    n_teach, n_crop, near = t_bf.shape[0], x_bf.shape[0], lax.axis_size(NEAR)
    own_crops = n_crop // near
    image_here = crop_image - lax.axis_index(DP) * img_local
    first_at, second_at = GLOBALS * image_here, GLOBALS * image_here + 1
    keep_first = (crop_global != 0).astype(jnp.float32)
    keep_second = (crop_global != 1).astype(jnp.float32)
    prep = (first_at, second_at, keep_first, keep_second, keep_first + keep_second)
    first_at, second_at, keep_first, keep_second, count = lax.optimization_barrier(prep)
    keep_first, keep_second, count = keep_first[:, None], keep_second[:, None], count[:, None]
    for step in range(ITERS):
        part_col = jnp.sum(q_mat, axis=0)
        col_tot = spread_sum(part_col, DP)
        q_mat = q_mat / col_tot[None, :] / total_protos
        part_row = jnp.sum(q_mat, axis=1)
        if step == 0:
            own = jnp.pad(part_total.reshape(near, -1), ((0, 0), (0, -own_crops % 128)))
            rows = jnp.broadcast_to(part_row[None], (near, n_teach))
            sent = jnp.concatenate([rows, own], axis=1).reshape(near, -1, 128)
            both = spread_sum(jnp.sum(lax.all_to_all(sent, NEAR, 0, 0), axis=0), "zh")
            row_tot = both[:n_teach]
        elif step == 1:
            both, part_row = lax.optimization_barrier((both, part_row))
            sent = jnp.concatenate([part_row, both[n_teach:]])
            both = spread(sent.reshape(-1, 128), NEAR)
            near_row = jnp.sum(both.reshape(near, -1)[:, :n_teach], axis=0)
            row_tot = spread_sum(near_row, "zh")
        else:
            near_row = spread_sum(part_row, NEAR)
            late = (near_row, both, first_at, second_at)
            near_row, both, first_at, second_at = lax.optimization_barrier(late)
            total = both.reshape(near, -1)[:, n_teach : n_teach + own_crops].reshape(-1)
            first = q_mat.at[first_at].get(mode="promise_in_bounds")
            second = q_mat.at[second_at].get(mode="promise_in_bounds")
            row_tot = spread_sum(near_row, "zh")
        if step + 1 < ITERS:
            q_mat = q_mat / row_tot[:, None] / teach_total
    teach_ids = lax.broadcasted_iota(jnp.int32, (1, n_teach), 1)

    def of_crop(index):
        return jnp.sum(jnp.where(index[:, None] == teach_ids, row_tot[None], 0.0), axis=1)

    first = first / of_crop(first_at)[:, None] / teach_total * teach_total
    second = second / of_crop(second_at)[:, None] / teach_total * teach_total
    probs = expo / total[:, None]
    target_rows = first * keep_first + second * keep_second
    scale_out = total_protos / 64.0
    grad_bf = (scale_out * (count * probs - target_rows) / 0.1).astype(jnp.bfloat16)
    dxn = lax.dot_general(
        grad_bf, w_bf, (((1,), (1,)), ((), ())), preferred_element_type=jnp.float32
    )
    dxn = dxn - x_norm * jnp.sum(x_norm * dxn, axis=1, keepdims=True)
    got = swap(dxn.astype(jnp.float16), "y")
    dxn = jnp.sum(got.astype(jnp.float32), axis=0)
    got = swap(dxn.astype(jnp.float16), "zl")
    dxn = jnp.sum(got.astype(jnp.float32), axis=0)
    dxn, grad_bf = lax.optimization_barrier((dxn, grad_bf))
    dwn_part = lax.dot_general(
        x_bf, grad_bf, (((0,), (0,)), ((), ())), preferred_element_type=jnp.float32
    )
    dwn_ring = dwn_reduce(dwn_part)
    got = spread(dxn.astype(jnp.float16), "zh")
    dxn = jnp.sum(got.astype(jnp.float32), axis=0).astype(jnp.float16)
    got = spread(dxn, "zl")
    dxn, dwn_ring = lax.optimization_barrier((got.reshape(-1, dxn.shape[1]), dwn_ring))
    got = spread(dxn, "y")
    dxn = got.reshape(-1, dxn.shape[1])
    dwn_total = dwn_join(dwn_ring)
    student_grad = x_scale * dxn.astype(jnp.float32)
    proto_grad = col_scale * (
        dwn_total - w_norm * jnp.sum(w_norm * dwn_total, axis=0, keepdims=True)
    )
    return (student_grad, proto_grad)


def solution(mesh):
    nx, ny, nzl = 4, 4, 4
    dp, proto = mesh.devices.shape
    split = (nx, dp // nx, ny, proto // ny // nzl, nzl)
    fine = Mesh(mesh.devices.reshape(split), ("x", "core", "y", "zh", "zl"))
    placed = (P(DP, None), P(DP, None), P(None, PROTO), P(DP), P(DP))

    return jax.shard_map(
        on_device,
        mesh=fine,
        in_specs=placed,
        out_specs=(P(DP, None), P(None, PROTO)),
        check_vma=False,
    )
```

```python
import jax
import jax.numpy as jnp
from jax import lax
from jax.sharding import Mesh, PartitionSpec as P


GLOBALS = 2
ITERS = 3
DP = ("x", "core")
PROTO = ("y", "zh", "zl")
NEAR = ("y", "zl")


def unit_rows(rows):
    scale = lax.rsqrt(jnp.sum(rows * rows, axis=1, keepdims=True) + 1e-06)
    return (rows * scale, scale)


def spread(part, axes):
    n = lax.axis_size(axes)
    return lax.all_to_all(jnp.broadcast_to(part[None], (n,) + part.shape), axes, 0, 0)


def swap(part, axes):
    n = lax.axis_size(axes)
    pieces = part.reshape((n, part.shape[0] // n) + part.shape[1:])
    return lax.all_to_all(pieces, axes, 0, 0)


def spread_sum(part, *stages):
    rows = part.reshape(-1, 128)
    for axes in stages:
        rows = jnp.sum(spread(rows, axes), axis=0)
    return rows.reshape(-1)


def shifted(part, axis, step):
    n = lax.axis_size(axis)
    return lax.ppermute(part, axis, [(i, (i + step) % n) for i in range(n)])


def dwn_reduce(part):
    core, x, nx = lax.axis_index("core"), lax.axis_index("x"), lax.axis_size("x")
    half = part.shape[0] // 2
    piece = half // nx

    def rows(arr, start, size):
        return lax.dynamic_slice_in_dim(arr, start * size, size, 0)

    mine = rows(part, core, half) + shifted(rows(part, 1 - core, half), "core", 1)
    sums = [rows(mine, x, piece)]
    for step in range(1, nx):
        sums.append(shifted(rows(mine, (x + step) % nx, piece), "x", step))
    own = lax.optimization_barrier(sum(sums[1:], sums[0]))
    got = [own] + [shifted(own, "x", step) for step in range(1, nx)]
    back = got[:1] + got[:0:-1]
    return jnp.concatenate(back + back, axis=0)


def dwn_join(ring):
    core, x, nx = lax.axis_index("core"), lax.axis_index("x"), lax.axis_size("x")
    half = ring.shape[0] // 2
    mine = lax.dynamic_slice_in_dim(ring, (nx - x) % nx * (half // nx), half, 0)
    other = shifted(mine, "core", 1)
    low, high = jnp.where(core == 0, mine, other), jnp.where(core == 0, other, mine)
    return jnp.concatenate([low, high], axis=0)


def on_device(student_rows, teacher_rows, prototypes, crop_image, crop_global):
    total_protos = lax.axis_size(PROTO) * prototypes.shape[1]
    img_local = teacher_rows.shape[0] // GLOBALS
    teach_total = lax.axis_size(DP) * teacher_rows.shape[0]
    weights = prototypes.astype(jnp.float32)
    col_scale = lax.rsqrt(jnp.sum(weights * weights, axis=0, keepdims=True) + 1e-06)
    w_norm = weights * col_scale
    w_bf = w_norm.astype(jnp.bfloat16)
    t_norm, _ = unit_rows(teacher_rows.astype(jnp.float32))
    t_bf = t_norm.astype(jnp.bfloat16)
    x_norm, x_scale = unit_rows(student_rows.astype(jnp.float32))
    x_bf = x_norm.astype(jnp.bfloat16)
    logits = jnp.dot(x_bf, w_bf, preferred_element_type=jnp.float32) / 0.1
    expo = jnp.exp(logits)
    part_total = jnp.sum(expo, axis=1)
    q_mat = jnp.exp(jnp.dot(t_bf, w_bf, preferred_element_type=jnp.float32) / 0.07)
    n_teach, n_crop, near = t_bf.shape[0], x_bf.shape[0], lax.axis_size(NEAR)
    own_crops = n_crop // near
    image_here = crop_image - lax.axis_index(DP) * img_local
    first_at, second_at = GLOBALS * image_here, GLOBALS * image_here + 1
    keep_first = (crop_global != 0).astype(jnp.float32)
    keep_second = (crop_global != 1).astype(jnp.float32)
    prep = (first_at, second_at, keep_first, keep_second, keep_first + keep_second)
    first_at, second_at, keep_first, keep_second, count = lax.optimization_barrier(prep)
    keep_first, keep_second, count = keep_first[:, None], keep_second[:, None], count[:, None]
    for step in range(ITERS):
        part_col = jnp.sum(q_mat, axis=0)
        col_tot = spread_sum(part_col, DP)
        q_mat = q_mat / col_tot[None, :] / total_protos
        part_row = jnp.sum(q_mat, axis=1)
        if step == 0:
            own = jnp.pad(part_total.reshape(near, -1), ((0, 0), (0, -own_crops % 128)))
            rows = jnp.broadcast_to(part_row[None], (near, n_teach))
            sent = jnp.concatenate([rows, own], axis=1).reshape(near, -1, 128)
            both = spread_sum(jnp.sum(lax.all_to_all(sent, NEAR, 0, 0), axis=0), "zh")
            row_tot = both[:n_teach]
        elif step == 1:
            both, part_row = lax.optimization_barrier((both, part_row))
            sent = jnp.concatenate([part_row, both[n_teach:]])
            both = spread(sent.reshape(-1, 128), NEAR)
            near_row = jnp.sum(both.reshape(near, -1)[:, :n_teach], axis=0)
            row_tot = spread_sum(near_row, "zh")
        else:
            near_row = spread_sum(part_row, NEAR)
            late = (near_row, both, first_at, second_at)
            near_row, both, first_at, second_at = lax.optimization_barrier(late)
            total = both.reshape(near, -1)[:, n_teach : n_teach + own_crops].reshape(-1)
            first = q_mat.at[first_at].get(mode="promise_in_bounds")
            second = q_mat.at[second_at].get(mode="promise_in_bounds")
            row_tot = spread_sum(near_row, "zh")
        if step + 1 < ITERS:
            q_mat = q_mat / row_tot[:, None] / teach_total
    teach_ids = lax.broadcasted_iota(jnp.int32, (1, n_teach), 1)

    def of_crop(index):
        return jnp.sum(jnp.where(index[:, None] == teach_ids, row_tot[None], 0.0), axis=1)

    first = first / of_crop(first_at)[:, None] / teach_total * teach_total
    second = second / of_crop(second_at)[:, None] / teach_total * teach_total
    probs = expo / total[:, None]
    target_rows = first * keep_first + second * keep_second
    scale_out = total_protos / 64.0
    grad_bf = (scale_out * (count * probs - target_rows) / 0.1).astype(jnp.bfloat16)
    dxn = lax.dot_general(
        grad_bf, w_bf, (((1,), (1,)), ((), ())), preferred_element_type=jnp.float32
    )
    dxn = dxn - x_norm * jnp.sum(x_norm * dxn, axis=1, keepdims=True)
    got = swap(dxn.astype(jnp.float16), "y")
    dxn = jnp.sum(got.astype(jnp.float32), axis=0)
    got = swap(dxn.astype(jnp.float16), "zl")
    dxn = jnp.sum(got.astype(jnp.float32), axis=0)
    dxn, grad_bf = lax.optimization_barrier((dxn, grad_bf))
    dwn_part = lax.dot_general(
        x_bf, grad_bf, (((0,), (0,)), ((), ())), preferred_element_type=jnp.float32
    )
    dwn_ring = dwn_reduce(dwn_part)
    got = spread(dxn.astype(jnp.float16), "zh")
    dxn = jnp.sum(got.astype(jnp.float32), axis=0).astype(jnp.float16)
    dxn, dwn_ring = lax.optimization_barrier((dxn, dwn_ring))
    got = spread(dxn, NEAR)
    dxn = got.reshape(-1, dxn.shape[1])
    dwn_total = dwn_join(dwn_ring)
    student_grad = x_scale * dxn.astype(jnp.float32)
    proto_grad = col_scale * (
        dwn_total - w_norm * jnp.sum(w_norm * dwn_total, axis=0, keepdims=True)
    )
    return (student_grad, proto_grad)


def solution(mesh):
    nx, ny, nzl = 4, 4, 4
    dp, proto = mesh.devices.shape
    split = (nx, dp // nx, ny, proto // ny // nzl, nzl)
    fine = Mesh(mesh.devices.reshape(split), ("x", "core", "y", "zh", "zl"))
    placed = (P(DP, None), P(DP, None), P(None, PROTO), P(DP), P(DP))

    return jax.shard_map(
        on_device,
        mesh=fine,
        in_specs=placed,
        out_specs=(P(DP, None), P(None, PROTO)),
        check_vma=False,
    )
```
